32 devices in a mesh: groups: 2 (over y), rows: 16 (over z, x, core).
Axes of the slice: x: 2, y: 2, z: 4, core: 2. Of those that a mesh axis runs over, the one named last changes fastest.
Arguments:
- latent: bfloat16 [64, 256, 512], P(('groups', 'rows')), parts along dimension 0, may hold values from -100 to 100
- gain_in: float32 [512], replicated, may hold values from 0.1 to 1.9
- shift_in: float32 [512], replicated, may hold values from -3 to 3
- conv_in: bfloat16 [4608, 256], replicated, may hold values from -0.09375 to 0.09375
- gain_mid: float32 [256], replicated, may hold values from 0.1 to 1.9
- shift_mid: float32 [256], replicated, may hold values from -3 to 3
- conv_mid: bfloat16 [2304, 256], replicated, may hold values from -0.125 to 0.125
- skip_weight: bfloat16 [512, 256], replicated, may hold values from -0.25 to 0.25
Outputs:
- decoded: bfloat16 [128, 512, 256], P(('groups', 'rows')), parts along dimension 0
The draws below stay inside these ranges and needn't reach their ends.
There are 2 independent parts, one for each index of `groups`. The reference program is written for one: setup_inputs(seed, part) draws one part's arguments, and reference() takes and returns one part's arrays. A program takes and returns all parts, laid end to end along the dimension named above; an argument that names none is the same for every part. Nothing has to cross between parts.
All inputs are finite; a program needn't handle non-finite values.
Results may differ from the reference program's by a relative error of at most 0.009.
Values may be sent and summed in bfloat16 or wider, within the bound.
No kernel may reach another device: no remote copies, remote signals or barrier semaphores. Data moves between devices by JAX's collectives and lax.ppermute only.
A program may use at most 64 MiB of HBM per device.

```python
import math
import jax
import jax.numpy as jnp
from jax import lax

C_IN = 512
C_OUT = 256
GROUPS = 32
R_IN = 2
W_IN = 256
H_IN = 32


def draw_latent(key, part):
    subkeys = jax.random.split(key, 4)
    noise = jnp.clip(jax.random.normal(subkeys[0], (H_IN, W_IN, C_IN), jnp.float32), -4.0, 4.0)
    position = jnp.arange(H_IN, dtype=jnp.float32) / max(H_IN - 1, 1)
    row_scale = jnp.exp(position * math.log(3.0) + jax.random.uniform(subkeys[1], (H_IN,), jnp.float32, 0.0, math.log(3.3)))
    band_parity = (jnp.arange(H_IN, dtype=jnp.int32) // R_IN % 2).astype(jnp.float32)
    row_scale = row_scale * (1.0 - 0.75 * band_parity)
    col_scale = jnp.exp(jax.random.uniform(subkeys[2], (W_IN,), jnp.float32, 0.0, math.log(10.0)))
    chan_scale = jnp.exp(jax.random.uniform(subkeys[3], (C_IN,), jnp.float32, math.log(0.5), math.log(2.0)))
    value = 0.1 * noise * row_scale[:, None, None] * col_scale[None, :, None] * chan_scale[None, None, :]
    return value.astype(jnp.bfloat16)


def normal_values(stream_key, dims, scale, reach, kind=jnp.bfloat16):
    values = scale * jax.random.normal(stream_key, dims, jnp.float32)
    return jnp.clip(values, min=-reach, max=reach).astype(kind)


def setup_inputs(seed: int = 0, part: int = 0) -> dict:
    splits = jax.random.split(jax.random.key(seed), 9)
    part_splits = jax.random.split(jax.random.fold_in(splits[8], part), 9)
    latent = draw_latent(jax.random.fold_in(jax.random.fold_in(splits[8], part), 71), part)
    gain_in = jnp.clip(1.0 + 0.18 * jax.random.normal(splits[1], (C_IN,), jnp.float32), 0.1, 1.9)
    shift_in = normal_values(splits[2], (C_IN,), 0.5, 3.0, jnp.float32)
    conv_in = normal_values(splits[3], (9 * C_IN, C_OUT), (9 * C_IN) ** -0.5, 0.09375)
    gain_mid = jnp.clip(1.0 + 0.18 * jax.random.normal(splits[4], (C_OUT,), jnp.float32), 0.1, 1.9)
    shift_mid = normal_values(splits[5], (C_OUT,), 0.5, 3.0, jnp.float32)
    conv_mid = normal_values(splits[6], (9 * C_OUT, C_OUT), (9 * C_OUT) ** -0.5, 0.125)
    skip_weight = normal_values(splits[7], (C_IN, C_OUT), C_IN ** -0.5, 0.25)
    return dict(latent=latent, gain_in=gain_in, shift_in=shift_in, conv_in=conv_in, gain_mid=gain_mid, shift_mid=shift_mid, conv_mid=conv_mid, skip_weight=skip_weight)


def group_norm(values, gain, shift):
    height, breadth, chans = values.shape
    grouped = values.reshape(height * breadth, GROUPS, chans // GROUPS)
    center = lax.optimization_barrier(jnp.mean(grouped, axis=(0, 2)))
    deviate = grouped - center[None, :, None]
    spread = lax.optimization_barrier(jnp.mean(deviate * deviate, axis=(0, 2)))
    normed = deviate / jnp.sqrt(spread[None, :, None] + 1e-06)
    return normed.reshape(height, breadth, chans) * gain + shift

def convolve(values, weight):
    height, breadth, chans = values.shape
    padded = jnp.pad(values, ((1, 1), (1, 1), (0, 0)))
    accum = jnp.zeros((height * breadth, weight.shape[1]), jnp.float32)
    for offset_index in range(9):
        shift_row = offset_index // 3
        shift_col = offset_index % 3
        window = padded[shift_row:shift_row + height, shift_col:shift_col + breadth].reshape(-1, chans)
        accum = accum + jnp.dot(window, weight[offset_index * chans:(offset_index + 1) * chans], preferred_element_type=jnp.float32)
    return accum.reshape(height, breadth, -1)

def reference(latent, gain_in, shift_in, conv_in, gain_mid, shift_mid, conv_mid, skip_weight):
    act = jax.nn.silu(group_norm(latent.astype(jnp.float32), gain_in, shift_in)).astype(jnp.bfloat16)
    upsampled = jnp.repeat(jnp.repeat(act, 2, axis=0), 2, axis=1)
    hidden = convolve(upsampled, conv_in).astype(jnp.bfloat16)
    middle = jax.nn.silu(group_norm(hidden.astype(jnp.float32), gain_mid, shift_mid)).astype(jnp.bfloat16)
    height, breadth, chans = upsampled.shape
    skipped = jnp.dot(upsampled.reshape(-1, chans), skip_weight, preferred_element_type=jnp.float32).reshape(height, breadth, -1)
    return (convolve(middle, conv_mid) + skipped).astype(jnp.bfloat16)
```

```python
import functools

import jax
import jax.numpy as jnp
from jax import lax
from jax.experimental import pallas as pl
from jax.experimental.pallas import tpu as pltpu
from jax.sharding import PartitionSpec as P

GROUPS = 32
EPS = 1e-06
F32 = jnp.float32
BF16 = jnp.bfloat16
LANES = 128
VMEM = pltpu.VMEM


def vmem_spec():
    return pl.BlockSpec(memory_space=VMEM)


def params(limit_mib):
    return pltpu.CompilerParams(vmem_limit_bytes=limit_mib << 20)


def cost(flops, data):
    return pl.CostEstimate(flops=flops, bytes_accessed=data, transcendentals=0)


def stack_lanes(row):
    count = row.shape[1] // LANES
    return [row[:, i * LANES : (i + 1) * LANES] for i in range(count)]


def put_stats(out_ref, total, square):
    rows = stack_lanes(total) + stack_lanes(square)
    fill = 8 - len(rows)
    if fill:
        rows.append(jnp.zeros((fill, LANES), F32))
    tile = jnp.concatenate(rows, axis=0)
    out_ref[...] = jnp.broadcast_to(tile[None], out_ref.shape)


def get_affine(stats_ref, gain, shift, group_width, count):
    chans = gain.shape[1]
    half = chans // LANES
    total = jnp.sum(stats_ref[...], axis=0)
    left = lax.broadcasted_iota(jnp.int32, (LANES, LANES), 0) // group_width
    right = lax.broadcasted_iota(jnp.int32, (LANES, LANES), 1) // group_width
    same = (left == right).astype(F32)
    pooled = jnp.dot(total, same, preferred_element_type=F32, precision=lax.Precision.HIGHEST)
    scaled = pooled * (1.0 / count)
    center = jnp.concatenate([scaled[i : i + 1] for i in range(half)], axis=1)
    moment = jnp.concatenate([scaled[half + i : half + i + 1] for i in range(half)], axis=1)
    spread = jnp.maximum(moment - center * center, 0.0)
    scale = gain * lax.rsqrt(spread + EPS)
    return 0.5 * scale, 0.5 * (shift - center * scale)


def half_silu(values, scale, offset):
    halved = values * scale + offset
    return halved + halved * jnp.tanh(halved)


def shift_rows(values, step):
    size = values.shape[0]
    moved = pltpu.roll(values, step % size, 0)
    place = lax.broadcasted_iota(jnp.int32, (size, 1), 0)
    edge = 0 if step == 1 else size - 1
    return jnp.where(place == edge, 0.0, moved)


def stats_kernel(latent_ref, out_ref):
    values = latent_ref[...].astype(F32)
    values = values.reshape(-1, values.shape[-1])
    put_stats(
        out_ref,
        jnp.sum(values, axis=0, keepdims=True),
        jnp.sum(values * values, axis=0, keepdims=True),
    )


def combine_kernel(weight_ref, out_ref):
    chans = out_ref.shape[1] // 4
    step = 16

    def pairs(taps):
        return (taps[0], taps[1] + taps[2]), (taps[0] + taps[1], taps[2])

    @pl.loop(0, chans // step)
    def _(index):
        start = pl.multiple_of(index * step, step)
        taps = [
            [weight_ref[pl.ds((3 * a + b) * chans + start, step), :].astype(F32) for b in range(3)]
            for a in range(3)
        ]
        columns = [pairs([taps[a][b] for a in range(3)]) for b in range(3)]
        for row_phase in range(2):
            for row_tap in range(2):
                across = pairs([columns[b][row_phase][row_tap] for b in range(3)])
                for col_phase in range(2):
                    for col_tap in range(2):
                        out_ref[
                            2 * row_phase + col_phase,
                            pl.ds((2 * row_tap + col_tap) * chans + start, step),
                            :,
                        ] = across[col_phase][col_tap].astype(BF16)


def first_conv(act_ref, weights_ref, row_phase, col_phase, first, count):
    wide = act_ref.shape[2] // 3
    window = pl.ds(col_phase * wide, 2 * wide)
    lhs = jnp.concatenate(
        [
            act_ref[first + tap : first + tap + count, :, window].reshape(-1, 2 * wide)
            for tap in range(2)
        ],
        axis=1,
    )
    return jnp.dot(lhs, weights_ref[2 * row_phase + col_phase], preferred_element_type=F32)


def hidden_kernel(
    count,
    axis_count,
    stats_ref,
    up_ref,
    latent_ref,
    down_ref,
    gain_ref,
    shift_ref,
    weights_ref,
    act_ref,
    hidden_ref,
    out_ref,
):
    rows, cols, chans = latent_ref.shape
    scale, offset = get_affine(stats_ref, gain_ref[...], shift_ref[...], chans // GROUPS, count)
    place = lax.axis_index("rows")
    for row in range(rows + 2):
        if row == 0:
            source, keep = up_ref[0], place > 0
        elif row == rows + 1:
            source, keep = down_ref[0], place < axis_count - 1
        else:
            source, keep = latent_ref[row - 1], None
        act = half_silu(source.astype(F32), scale, offset)
        if keep is not None:
            act = act * keep.astype(F32)
        act_ref[row, :, 0:chans] = shift_rows(act, 1).astype(BF16)
        act_ref[row, :, chans : 2 * chans] = act.astype(BF16)
        act_ref[row, :, 2 * chans :] = shift_rows(act, -1).astype(BF16)
    totals, squares = [], []
    for row_phase in range(2):
        for col_phase in range(2):
            found = first_conv(act_ref, weights_ref, row_phase, col_phase, row_phase, rows)
            found = found.astype(BF16)
            for row in range(rows):
                hidden_ref[2 * row + row_phase, col_phase] = found[row * cols : (row + 1) * cols]
            wide = found.astype(F32)
            totals.append(jnp.sum(wide, axis=0, keepdims=True))
            squares.append(jnp.sum(wide * wide, axis=0, keepdims=True))
    put_stats(out_ref, sum(totals[1:], totals[0]), sum(squares[1:], squares[0]))


def border_kernel(act_ref, weights_ref, skip_ref, border_ref, skipped_ref):
    rows = act_ref.shape[0] - 2
    wide = act_ref.shape[2] // 3
    for col_phase in range(2):
        border_ref[0, col_phase] = first_conv(act_ref, weights_ref, 1, col_phase, 0, 1).astype(BF16)
        border_ref[1, col_phase] = first_conv(act_ref, weights_ref, 0, col_phase, rows, 1).astype(
            BF16
        )
    middle = act_ref[1 : 1 + rows, :, wide : 2 * wide].reshape(-1, wide)
    skipped_ref[...] = jnp.dot(middle, skip_ref[...], preferred_element_type=F32)


def output_kernel(
    count,
    axis_count,
    stats_ref,
    border_ref,
    hidden_ref,
    gain_ref,
    shift_ref,
    weight_ref,
    skipped_ref,
    out_ref,
    mid_ref,
    mixed_ref,
):
    rows, _, cols, chans = hidden_ref.shape
    scale, offset = get_affine(stats_ref, gain_ref[...], shift_ref[...], chans // GROUPS, count)
    place = lax.axis_index("rows")
    for row in range(rows + 2):
        pair = []
        for phase in range(2):
            if row == 0:
                source, keep = border_ref[0, phase], place > 0
            elif row == rows + 1:
                source, keep = border_ref[1, phase], place < axis_count - 1
            else:
                source, keep = hidden_ref[row - 1, phase], None
            value = half_silu(source.astype(F32), scale, offset)
            if keep is not None:
                value = value * keep.astype(F32)
            pair.append(value)
        even, odd = pair
        mid_ref[row, :, 0:chans] = shift_rows(odd, 1).astype(BF16)
        mid_ref[row, :, chans : 2 * chans] = even.astype(BF16)
        mid_ref[row, :, 2 * chans : 3 * chans] = odd.astype(BF16)
        mid_ref[row, :, 3 * chans :] = shift_rows(even, -1).astype(BF16)
    for row in range(rows):
        base = skipped_ref[pl.ds((row // 2) * cols, cols), :]
        for phase in range(2):
            lhs = jnp.concatenate(
                [mid_ref[row + tap, :, phase * chans : (phase + 3) * chans] for tap in range(3)],
                axis=1,
            )
            found = base + jnp.dot(lhs, weight_ref[...], preferred_element_type=F32)
            for part in range(chans // LANES):
                mixed_ref[part, pl.ds(phase, cols, stride=2), :] = found[
                    :, part * LANES : (part + 1) * LANES
                ]
        for part in range(chans // LANES):
            out_ref[row, :, part * LANES : (part + 1) * LANES] = mixed_ref[part].astype(BF16)


def body(latent, gain_in, shift_in, conv_in, gain_mid, shift_mid, conv_mid, skip_weight):
    axis = "rows"
    peers = lax.axis_size(axis)
    rows, cols, chans = latent.shape
    outs = conv_in.shape[1]
    ends = peers - 1
    up = lax.ppermute(latent[rows - 1 :], axis, [(i, i + 1) for i in range(ends)])
    down = lax.ppermute(latent[:1], axis, [(i + 1, i) for i in range(ends)])

    stats = pl.pallas_call(
        stats_kernel,
        out_shape=jax.ShapeDtypeStruct((peers, 8, LANES), F32),
        in_specs=[vmem_spec()],
        out_specs=vmem_spec(),
        compiler_params=params(16),
        name="stats",
    )(latent)
    stats = lax.all_to_all(stats, axis, 0, 0)

    weights = pl.pallas_call(
        combine_kernel,
        out_shape=jax.ShapeDtypeStruct((4, 4 * chans, outs), BF16),
        in_specs=[vmem_spec()],
        out_specs=vmem_spec(),
        compiler_params=params(16),
        cost_estimate=cost(4 << 20, 8 << 20),
        name="combine",
    )(conv_in)

    act, hidden, stats_mid = pl.pallas_call(
        functools.partial(
            hidden_kernel, float(rows * cols * (chans // GROUPS) * peers), peers
        ),
        out_shape=(
            jax.ShapeDtypeStruct((rows + 2, cols, 3 * chans), BF16),
            jax.ShapeDtypeStruct((2 * rows, 2, cols, outs), BF16),
            jax.ShapeDtypeStruct((peers, 8, LANES), F32),
        ),
        in_specs=[vmem_spec()] * 7,
        out_specs=(vmem_spec(),) * 3,
        compiler_params=params(24),
        name="hidden",
    )(stats, up, latent, down, gain_in.reshape(1, -1), shift_in.reshape(1, -1), weights)
    stats_mid = lax.all_to_all(stats_mid, axis, 0, 0)

    border, skipped = pl.pallas_call(
        border_kernel,
        out_shape=(
            jax.ShapeDtypeStruct((2, 2, cols, outs), BF16),
            jax.ShapeDtypeStruct((rows * cols, outs), F32),
        ),
        in_specs=[vmem_spec()] * 3,
        out_specs=(vmem_spec(),) * 2,
        compiler_params=params(24),
        cost_estimate=cost(1200 << 20, 8 << 20),
        name="border",
    )(act, weights, skip_weight)

    return pl.pallas_call(
        functools.partial(
            output_kernel, float(4 * rows * cols * (outs // GROUPS) * peers), peers
        ),
        out_shape=jax.ShapeDtypeStruct((2 * rows, 2 * cols, outs), BF16),
        in_specs=[vmem_spec()] * 7,
        out_specs=vmem_spec(),
        scratch_shapes=[
            VMEM((2 * rows + 2, cols, 4 * outs), BF16),
            VMEM((outs // LANES, 2 * cols, LANES), F32),
        ],
        compiler_params=params(24),
        name="output",
    )(
        stats_mid,
        border,
        hidden,
        gain_mid.reshape(1, -1),
        shift_mid.reshape(1, -1),
        conv_mid,
        skipped,
    )


def solution(mesh):
    placed = (P(("groups", "rows"), None, None), P(), P(), P(), P(), P(), P(), P())
    return jax.shard_map(
        body,
        mesh=mesh,
        in_specs=placed,
        out_specs=P(("groups", "rows"), None, None),
        check_vma=False,
    )
```

```python
import functools

import jax
import jax.numpy as jnp
from jax import lax
from jax.experimental import pallas as pl
from jax.experimental.pallas import tpu as pltpu
from jax.sharding import PartitionSpec as P

GROUPS = 32
EPS = 1e-06
F32 = jnp.float32
BF16 = jnp.bfloat16
LANES = 128
PARTS = 4
VMEM = pltpu.VMEM


def vmem_spec():
    return pl.BlockSpec(memory_space=VMEM)


def in_hbm(values):
    return pltpu.with_memory_space_constraint(values, pltpu.HBM)


def params(limit_mib):
    return pltpu.CompilerParams(vmem_limit_bytes=limit_mib << 20)


def cost(flops, data):
    return pl.CostEstimate(flops=flops, bytes_accessed=data, transcendentals=0)


def stack_lanes(row):
    count = row.shape[1] // LANES
    return [row[:, i * LANES : (i + 1) * LANES] for i in range(count)]


def put_stats(out_ref, total, square):
    rows = stack_lanes(total) + stack_lanes(square)
    fill = 8 - len(rows)
    if fill:
        rows.append(jnp.zeros((fill, LANES), F32))
    tile = jnp.concatenate(rows, axis=0)
    out_ref[...] = jnp.broadcast_to(tile[None], out_ref.shape)


def get_affine(stats_ref, gain, shift, group_width, count):
    chans = gain.shape[1]
    half = chans // LANES
    total = jnp.sum(stats_ref[...], axis=0)
    left = lax.broadcasted_iota(jnp.int32, (LANES, LANES), 0) // group_width
    right = lax.broadcasted_iota(jnp.int32, (LANES, LANES), 1) // group_width
    same = (left == right).astype(F32)
    pooled = jnp.dot(total, same, preferred_element_type=F32, precision=lax.Precision.HIGHEST)
    scaled = pooled * (1.0 / count)
    center = jnp.concatenate([scaled[i : i + 1] for i in range(half)], axis=1)
    moment = jnp.concatenate([scaled[half + i : half + i + 1] for i in range(half)], axis=1)
    spread = jnp.maximum(moment - center * center, 0.0)
    scale = gain * lax.rsqrt(spread + EPS)
    return 0.5 * scale, 0.5 * (shift - center * scale)


def half_silu(values, scale, offset):
    halved = values * scale + offset
    return halved + halved * jnp.tanh(halved)


def shift_rows(values, step):
    size = values.shape[0]
    moved = pltpu.roll(values, step % size, 0)
    place = lax.broadcasted_iota(jnp.int32, (size, 1), 0)
    edge = 0 if step == 1 else size - 1
    return jnp.where(place == edge, 0.0, moved)


def stats_kernel(latent_ref, stats_ref, head_ref, tail_ref, held_ref, sems):
    rows = latent_ref.shape[0]
    copies = [
        pltpu.make_async_copy(latent_ref.at[row], held_ref.at[row], sems.at[row])
        for row in range(rows)
    ]
    for copy in copies:
        copy.start()
    total, square = 0.0, 0.0
    for row in range(rows):
        copies[row].wait()
        values = held_ref[row].astype(F32)
        total += jnp.sum(values, axis=0, keepdims=True)
        square += jnp.sum(values * values, axis=0, keepdims=True)
    put_stats(stats_ref, total, square)
    head_ref[0] = held_ref[0]
    tail_ref[0] = held_ref[rows - 1]


def combine_kernel(weight_ref, out_ref, held_ref, made_ref, in_sems, out_sems):
    step = 16
    chans = weight_ref.shape[1]
    width = chans // PARTS

    def pairs(taps):
        return (taps[0], taps[1] + taps[2]), (taps[0] + taps[1], taps[2])

    fetches, stores = [], []
    for index in range(PARTS):
        part = pl.ds(index * width, width)
        fetches.append(
            pltpu.make_async_copy(
                weight_ref.at[:, part, :], held_ref.at[:, part, :], in_sems.at[index]
            )
        )
        stores.append(
            pltpu.make_async_copy(
                made_ref.at[:, :, part, :], out_ref.at[:, :, part, :], out_sems.at[index]
            )
        )
    for fetch in fetches:
        fetch.start()
    for index in range(PARTS):
        fetches[index].wait()

        @pl.loop(0, width // step)
        def _(inner):
            part = pl.ds(pl.multiple_of(index * width + inner * step, step), step)
            columns = [
                pairs([held_ref[3 * a + b, part, :].astype(F32) for a in range(3)])
                for b in range(3)
            ]
            for row_phase in range(2):
                for row_tap in range(2):
                    across = pairs([columns[b][row_phase][row_tap] for b in range(3)])
                    for col_phase in range(2):
                        for col_tap in range(2):
                            made_ref[
                                2 * row_phase + col_phase, 2 * row_tap + col_tap, part, :
                            ] = across[col_phase][col_tap].astype(BF16)

        stores[index].start()
    for store in stores:
        store.wait()


def fill_act(out_ref, row, act):
    chans = act.shape[1]
    out_ref[row, :, 0:chans] = shift_rows(act, 1).astype(BF16)
    out_ref[row, :, chans : 2 * chans] = act.astype(BF16)
    out_ref[row, :, 2 * chans :] = shift_rows(act, -1).astype(BF16)


def first_conv(act_ref, weight_ref, col_phase, first, count):
    wide = act_ref.shape[2] // 3
    window = pl.ds(col_phase * wide, 2 * wide)
    lhs = jnp.concatenate(
        [
            act_ref[first + tap : first + tap + count, :, window].reshape(-1, 2 * wide)
            for tap in range(2)
        ],
        axis=1,
    )
    return jnp.dot(lhs, weight_ref[...], preferred_element_type=F32)


def fetch(weights_ref, held_ref, sems):
    copies = [
        pltpu.make_async_copy(weights_ref.at[phase], held_ref.at[phase], sems.at[phase])
        for phase in range(4)
    ]
    for copy in copies:
        copy.start()
    return copies


def hidden_kernel(
    count,
    axis_count,
    stats_ref,
    up_ref,
    latent_ref,
    down_ref,
    gain_ref,
    shift_ref,
    weights_ref,
    act_ref,
    hidden_ref,
    out_ref,
    shifted_ref,
    held_ref,
    sems,
):
    copies = fetch(weights_ref, held_ref, sems)
    rows, cols, chans = latent_ref.shape
    scale, offset = get_affine(stats_ref, gain_ref[...], shift_ref[...], chans // GROUPS, count)
    place = lax.axis_index("rows")
    for row in range(rows + 2):
        if row == 0:
            source, keep = up_ref[0], place > 0
        elif row == rows + 1:
            source, keep = down_ref[0], place < axis_count - 1
        else:
            source, keep = latent_ref[row - 1], None
        act = half_silu(source.astype(F32), scale, offset)
        if keep is not None:
            act = act * keep.astype(F32)
        act_ref[row] = act.astype(BF16)
        fill_act(shifted_ref, row, act)
    totals, squares = [], []
    for row_phase in range(2):
        for col_phase in range(2):
            phase = 2 * row_phase + col_phase
            copies[phase].wait()
            found = first_conv(shifted_ref, held_ref.at[phase], col_phase, row_phase, rows)
            found = found.astype(BF16)
            for row in range(rows):
                hidden_ref[2 * row + row_phase, col_phase] = found[row * cols : (row + 1) * cols]
            wide = found.astype(F32)
            totals.append(jnp.sum(wide, axis=0, keepdims=True))
            squares.append(jnp.sum(wide * wide, axis=0, keepdims=True))
    put_stats(out_ref, sum(totals[1:], totals[0]), sum(squares[1:], squares[0]))


def border_kernel(
    act_ref,
    weights_ref,
    skip_ref,
    border_ref,
    skipped_ref,
    shifted_ref,
    held_ref,
    skip_held_ref,
    sems,
    skip_sem,
):
    skip_copy = pltpu.make_async_copy(skip_ref, skip_held_ref, skip_sem)
    skip_copy.start()
    copies = fetch(weights_ref, held_ref, sems)
    total, cols, chans = act_ref.shape
    rows = total - 2
    for row in range(total):
        fill_act(shifted_ref, row, act_ref[row].astype(F32))
    skip_copy.wait()
    skipped_ref[...] = jnp.dot(
        act_ref[1 : 1 + rows].reshape(-1, chans), skip_held_ref[...], preferred_element_type=F32
    )
    for row_phase in range(2):
        side, first = (1, rows) if row_phase == 0 else (0, 0)
        for col_phase in range(2):
            phase = 2 * row_phase + col_phase
            copies[phase].wait()
            border_ref[side, col_phase] = first_conv(
                shifted_ref, held_ref.at[phase], col_phase, first, 1
            ).astype(BF16)


def output_kernel(
    count,
    axis_count,
    stats_ref,
    border_ref,
    hidden_ref,
    gain_ref,
    shift_ref,
    weight_ref,
    skipped_ref,
    out_ref,
    mid_ref,
    mixed_ref,
    done_ref,
    held_ref,
    sems,
    held_sem,
):
    fetched = pltpu.make_async_copy(weight_ref, held_ref, held_sem)
    fetched.start()
    rows, _, cols, chans = hidden_ref.shape
    scale, offset = get_affine(stats_ref, gain_ref[...], shift_ref[...], chans // GROUPS, count)
    place = lax.axis_index("rows")
    for row in range(rows + 2):
        pair = []
        for phase in range(2):
            if row == 0:
                source, keep = border_ref[0, phase], place > 0
            elif row == rows + 1:
                source, keep = border_ref[1, phase], place < axis_count - 1
            else:
                source, keep = hidden_ref[row - 1, phase], None
            value = half_silu(source.astype(F32), scale, offset)
            if keep is not None:
                value = value * keep.astype(F32)
            pair.append(value)
        even, odd = pair
        mid_ref[row, :, 0:chans] = shift_rows(odd, 1).astype(BF16)
        mid_ref[row, :, chans : 2 * chans] = even.astype(BF16)
        mid_ref[row, :, 2 * chans : 3 * chans] = odd.astype(BF16)
        mid_ref[row, :, 3 * chans :] = shift_rows(even, -1).astype(BF16)
    fetched.wait()
    copies = []
    for row in range(rows):
        base = skipped_ref[pl.ds((row // 2) * cols, cols), :]
        for phase in range(2):
            lhs = jnp.concatenate(
                [mid_ref[row + tap, :, phase * chans : (phase + 3) * chans] for tap in range(3)],
                axis=1,
            )
            found = base + jnp.dot(lhs, held_ref[...], preferred_element_type=F32)
            for part in range(chans // LANES):
                mixed_ref[part, pl.ds(phase, cols, stride=2), :] = found[
                    :, part * LANES : (part + 1) * LANES
                ]
        for part in range(chans // LANES):
            done_ref[row, :, part * LANES : (part + 1) * LANES] = mixed_ref[part].astype(BF16)
        copy = pltpu.make_async_copy(done_ref.at[row], out_ref.at[row], sems.at[row])
        copy.start()
        copies.append(copy)
    for copy in copies:
        copy.wait()


def body(latent, gain_in, shift_in, conv_in, gain_mid, shift_mid, conv_mid, skip_weight):
    axis = "rows"
    peers = lax.axis_size(axis)
    rows, cols, chans = latent.shape
    outs = conv_in.shape[1]
    ends = peers - 1
    taken = vmem_spec()
    far = pl.BlockSpec(memory_space=pltpu.HBM)
    dma = pltpu.SemaphoreType.DMA
    whole = jax.ShapeDtypeStruct

    with jax.named_scope("stats"):
        stats, head, tail = pl.pallas_call(
            stats_kernel,
            out_shape=(
                whole((peers, 8, LANES), F32),
                whole((1, cols, chans), BF16),
                whole((1, cols, chans), BF16),
            ),
            in_specs=[far],
            out_specs=(taken,) * 3,
            scratch_shapes=[VMEM(latent.shape, BF16), dma((rows,))],
            compiler_params=params(16),
            name="stats",
        )(in_hbm(latent))
    with jax.named_scope("exchange_in"):
        stats = lax.all_to_all(stats, axis, 0, 0)
    with jax.named_scope("halo"):
        up = lax.ppermute(tail, axis, [(i, i + 1) for i in range(ends)])
        down = lax.ppermute(head, axis, [(i + 1, i) for i in range(ends)])

    with jax.named_scope("combine"):
        weights = pl.pallas_call(
            combine_kernel,
            out_shape=pltpu.HBM((4, 4, chans, outs), BF16),
            in_specs=[far],
            out_specs=far,
            scratch_shapes=[
                VMEM((9, chans, outs), BF16),
                VMEM((4, 4, chans, outs), BF16),
                dma((PARTS,)),
                dma((PARTS,)),
            ],
            compiler_params=params(16),
            cost_estimate=cost(4 << 20, 8 << 20),
            name="combine",
        )(in_hbm(conv_in.reshape(9, chans, outs))).reshape(4, 4 * chans, outs)

    with jax.named_scope("hidden"):
        act, hidden, stats_mid = pl.pallas_call(
            functools.partial(
                hidden_kernel, float(rows * cols * (chans // GROUPS) * peers), peers
            ),
            out_shape=(
                whole((rows + 2, cols, chans), BF16),
                whole((2 * rows, 2, cols, outs), BF16),
                whole((peers, 8, LANES), F32),
            ),
            in_specs=[taken] * 6 + [far],
            out_specs=(taken,) * 3,
            scratch_shapes=[
                VMEM((rows + 2, cols, 3 * chans), BF16),
                VMEM((4, 4 * chans, outs), BF16),
                dma((4,)),
            ],
            compiler_params=params(24),
            name="hidden",
        )(stats, up, latent, down, gain_in.reshape(1, -1), shift_in.reshape(1, -1), in_hbm(weights))
    with jax.named_scope("exchange_mid"):
        stats_mid = lax.all_to_all(stats_mid, axis, 0, 0)

    with jax.named_scope("border"):
        border, skipped = pl.pallas_call(
            border_kernel,
            out_shape=(
                whole((2, 2, cols, outs), BF16),
                whole((rows * cols, outs), F32),
            ),
            in_specs=[taken, far, far],
            out_specs=(taken,) * 2,
            scratch_shapes=[
                VMEM((rows + 2, cols, 3 * chans), BF16),
                VMEM((4, 4 * chans, outs), BF16),
                VMEM((chans, outs), BF16),
                dma((4,)),
                dma,
            ],
            compiler_params=params(24),
            cost_estimate=cost(1200 << 20, 8 << 20),
            name="border",
        )(act, in_hbm(weights), in_hbm(skip_weight))

    with jax.named_scope("output"):
        return pl.pallas_call(
            functools.partial(
                output_kernel, float(4 * rows * cols * (outs // GROUPS) * peers), peers
            ),
            out_shape=whole((2 * rows, 2 * cols, outs), BF16),
            in_specs=[taken] * 5 + [far, taken],
            out_specs=far,
            scratch_shapes=[
                VMEM((2 * rows + 2, cols, 4 * outs), BF16),
                VMEM((outs // LANES, 2 * cols, LANES), F32),
                VMEM((2 * rows, 2 * cols, outs), BF16),
                VMEM(conv_mid.shape, BF16),
                dma((2 * rows,)),
                dma,
            ],
            compiler_params=params(24),
            name="output",
        )(
            stats_mid,
            border,
            hidden,
            gain_mid.reshape(1, -1),
            shift_mid.reshape(1, -1),
            in_hbm(conv_mid),
            skipped,
        )


def solution(mesh):
    placed = (P(("groups", "rows"), None, None), P(), P(), P(), P(), P(), P(), P())
    return jax.shard_map(
        body,
        mesh=mesh,
        in_specs=placed,
        out_specs=P(("groups", "rows"), None, None),
        check_vma=False,
    )
```

```python
import functools

import jax
import jax.numpy as jnp
from jax import lax
from jax.experimental import pallas as pl
from jax.experimental.pallas import tpu as pltpu
from jax.sharding import PartitionSpec as P

GROUPS = 32
EPS = 1e-06
F32 = jnp.float32
BF16 = jnp.bfloat16
LANES = 128
VMEM = pltpu.VMEM


def vmem_spec():
    return pl.BlockSpec(memory_space=VMEM)


def in_hbm(values):
    return pltpu.with_memory_space_constraint(values, pltpu.HBM)


def params(limit_mib):
    return pltpu.CompilerParams(vmem_limit_bytes=limit_mib << 20)


def cost(flops, data):
    return pl.CostEstimate(flops=flops, bytes_accessed=data, transcendentals=0)


def stack_lanes(row):
    count = row.shape[1] // LANES
    return [row[:, i * LANES : (i + 1) * LANES] for i in range(count)]


def put_stats(out_ref, total, square):
    rows = stack_lanes(total) + stack_lanes(square)
    fill = 8 - len(rows)
    if fill:
        rows.append(jnp.zeros((fill, LANES), F32))
    tile = jnp.concatenate(rows, axis=0)
    out_ref[...] = jnp.broadcast_to(tile[None], out_ref.shape)


def get_affine(stats_ref, gain, shift, group_width, count):
    chans = gain.shape[1]
    half = chans // LANES
    total = jnp.sum(stats_ref[...], axis=0)
    left = lax.broadcasted_iota(jnp.int32, (LANES, LANES), 0) // group_width
    right = lax.broadcasted_iota(jnp.int32, (LANES, LANES), 1) // group_width
    same = (left == right).astype(F32)
    pooled = jnp.dot(total, same, preferred_element_type=F32, precision=lax.Precision.HIGHEST)
    scaled = pooled * (1.0 / count)
    center = jnp.concatenate([scaled[i : i + 1] for i in range(half)], axis=1)
    moment = jnp.concatenate([scaled[half + i : half + i + 1] for i in range(half)], axis=1)
    spread = jnp.maximum(moment - center * center, 0.0)
    scale = gain * lax.rsqrt(spread + EPS)
    return 0.5 * scale, 0.5 * (shift - center * scale)


def half_silu(values, scale, offset):
    halved = values * scale + offset
    return halved + halved * jnp.tanh(halved)


def shift_rows(values, step):
    size = values.shape[0]
    moved = pltpu.roll(values, step % size, 0)
    place = lax.broadcasted_iota(jnp.int32, (size, 1), 0)
    edge = 0 if step == 1 else size - 1
    return jnp.where(place == edge, 0.0, moved)


def stats_kernel(latent_ref, stats_ref, head_ref, tail_ref, held_ref, sems):
    rows = latent_ref.shape[0]
    copies = [
        pltpu.make_async_copy(latent_ref.at[row], held_ref.at[row], sems.at[row])
        for row in range(rows)
    ]
    for copy in copies:
        copy.start()
    total, square = 0.0, 0.0
    for row in range(rows):
        copies[row].wait()
        values = held_ref[row].astype(F32)
        total += jnp.sum(values, axis=0, keepdims=True)
        square += jnp.sum(values * values, axis=0, keepdims=True)
    put_stats(stats_ref, total, square)
    head_ref[0] = held_ref[0]
    tail_ref[0] = held_ref[rows - 1]


def fetch_all(pairs, sems):
    copies = [
        pltpu.make_async_copy(source, target, sems.at[index])
        for index, (source, target) in enumerate(pairs)
    ]
    for copy in copies:
        copy.start()
    return copies


def hidden_kernel(
    count,
    axis_count,
    stats_ref,
    up_ref,
    latent_ref,
    down_ref,
    gain_ref,
    shift_ref,
    weight_ref,
    skip_ref,
    hidden_ref,
    out_ref,
    skipped_ref,
    act_ref,
    tap_ref,
    gains_ref,
    rows_ref,
    taps_ref,
    skips_ref,
    sems,
):
    rows, cols, chans = latent_ref.shape
    pairs = [(gain_ref, gains_ref.at[0]), (shift_ref, gains_ref.at[1]), (latent_ref, rows_ref)]
    order = [0, 1, 2, 6, 7, 8, 3, 4, 5]
    for tap in order:
        pairs.append((weight_ref.at[pl.ds(tap * chans, chans), :], taps_ref.at[tap]))
    pairs.append((skip_ref, skips_ref))
    copies = fetch_all(pairs, sems)
    copies[0].wait()
    copies[1].wait()
    scale, offset = get_affine(stats_ref, gains_ref[0], gains_ref[1], chans // GROUPS, count)
    place = lax.axis_index("rows")
    for row in [0, rows + 1] + list(range(1, rows + 1)):
        if row == 0:
            source, keep = up_ref[0], place > 0
        elif row == rows + 1:
            source, keep = down_ref[0], place < axis_count - 1
        else:
            if row == 1:
                copies[2].wait()
            source, keep = rows_ref[row - 1], None
        act = half_silu(source.astype(F32), scale, offset)
        if keep is not None:
            act = act * keep.astype(F32)
        act_ref[pl.ds(row * cols, cols), :] = act.astype(BF16)

    total_rows = 2 * rows + 2
    sources = [[(row + tap - 2) // 2 + 1 for tap in range(3)] for row in range(total_rows)]
    for index, tap in enumerate(order):
        copies[3 + index].wait()
        used = [source[tap // 3] for source in sources]
        first, last = min(used), max(used)
        part = pl.ds(first * cols, (last + 1 - first) * cols)
        tap_ref[tap, part, :] = jnp.dot(
            act_ref[part, :],
            taps_ref[tap],
            preferred_element_type=F32,
        )
    copies[12].wait()
    middle = act_ref[cols : (rows + 1) * cols, :]
    skipped_ref[...] = jnp.dot(middle, skips_ref[...], preferred_element_type=F32)

    totals, squares = [], []
    for row in range(total_rows):
        left, center, right = (
            sum(
                tap_ref[3 * a + b, pl.ds(sources[row][a] * cols, cols), :] for a in range(3)
            )
            for b in range(3)
        )
        pair = (
            shift_rows(left, 1) + (center + right),
            (left + center) + shift_rows(right, -1),
        )
        for phase in range(2):
            found = pair[phase].astype(BF16)
            hidden_ref[row, phase] = found
            if 0 < row < total_rows - 1:
                wide = found.astype(F32)
                totals.append(jnp.sum(wide, axis=0, keepdims=True))
                squares.append(jnp.sum(wide * wide, axis=0, keepdims=True))
    put_stats(out_ref, sum(totals[1:], totals[0]), sum(squares[1:], squares[0]))


def output_kernel(
    count,
    axis_count,
    stats_ref,
    hidden_ref,
    gain_ref,
    shift_ref,
    weight_ref,
    skipped_ref,
    out_ref,
    mid_ref,
    mixed_ref,
    done_ref,
    held_ref,
    gains_ref,
    sems,
    in_sems,
):
    fetches = fetch_all(
        [(gain_ref, gains_ref.at[0]), (shift_ref, gains_ref.at[1]), (weight_ref, held_ref)],
        in_sems,
    )
    total_rows, _, cols, chans = hidden_ref.shape
    rows = total_rows - 2
    fetches[0].wait()
    fetches[1].wait()
    scale, offset = get_affine(stats_ref, gains_ref[0], gains_ref[1], chans // GROUPS, count)
    place = lax.axis_index("rows")
    for row in range(rows + 2):
        pair = []
        keep = None
        if row == 0:
            keep = place > 0
        elif row == rows + 1:
            keep = place < axis_count - 1
        for phase in range(2):
            value = half_silu(hidden_ref[row, phase].astype(F32), scale, offset)
            if keep is not None:
                value = value * keep.astype(F32)
            pair.append(value)
        even, odd = pair
        mid_ref[row, :, 0:chans] = shift_rows(odd, 1).astype(BF16)
        mid_ref[row, :, chans : 2 * chans] = even.astype(BF16)
        mid_ref[row, :, 2 * chans : 3 * chans] = odd.astype(BF16)
        mid_ref[row, :, 3 * chans :] = shift_rows(even, -1).astype(BF16)
    fetches[2].wait()
    copies = []
    for row in range(rows):
        base = skipped_ref[pl.ds((row // 2) * cols, cols), :]
        for phase in range(2):
            lhs = jnp.concatenate(
                [mid_ref[row + tap, :, phase * chans : (phase + 3) * chans] for tap in range(3)],
                axis=1,
            )
            found = base + jnp.dot(lhs, held_ref[...], preferred_element_type=F32)
            for part in range(chans // LANES):
                mixed_ref[part, pl.ds(phase, cols, stride=2), :] = found[
                    :, part * LANES : (part + 1) * LANES
                ]
        for part in range(chans // LANES):
            done_ref[row, :, part * LANES : (part + 1) * LANES] = mixed_ref[part].astype(BF16)
        copy = pltpu.make_async_copy(done_ref.at[row], out_ref.at[row], sems.at[row])
        copy.start()
        copies.append(copy)
    for copy in copies:
        copy.wait()


def body(latent, gain_in, shift_in, conv_in, gain_mid, shift_mid, conv_mid, skip_weight):
    axis = "rows"
    peers = lax.axis_size(axis)
    rows, cols, chans = latent.shape
    outs = conv_in.shape[1]
    ends = peers - 1
    taken = vmem_spec()
    far = pl.BlockSpec(memory_space=pltpu.HBM)
    dma = pltpu.SemaphoreType.DMA
    whole = jax.ShapeDtypeStruct

    with jax.named_scope("stats"):
        stats, head, tail = pl.pallas_call(
            stats_kernel,
            out_shape=(
                whole((peers, 8, LANES), F32),
                whole((1, cols, chans), BF16),
                whole((1, cols, chans), BF16),
            ),
            in_specs=[far],
            out_specs=(taken,) * 3,
            scratch_shapes=[VMEM(latent.shape, BF16), dma((rows,))],
            compiler_params=params(16),
            name="stats",
        )(in_hbm(latent))
    with jax.named_scope("exchange_in"):
        stats = lax.all_to_all(stats, axis, 0, 0)
    with jax.named_scope("halo"):
        up = lax.ppermute(tail, axis, [(i, i + 1) for i in range(ends)])
        down = lax.ppermute(head, axis, [(i + 1, i) for i in range(ends)])

    with jax.named_scope("hidden"):
        hidden, stats_mid, skipped = pl.pallas_call(
            functools.partial(
                hidden_kernel, float(rows * cols * (chans // GROUPS) * peers), peers
            ),
            out_shape=(
                whole((2 * rows + 2, 2, cols, outs), BF16),
                whole((peers, 8, LANES), F32),
                whole((rows * cols, outs), F32),
            ),
            in_specs=[taken, taken, far, taken, far, far, far, far],
            out_specs=(taken,) * 3,
            scratch_shapes=[
                VMEM(((rows + 2) * cols, chans), BF16),
                VMEM((9, (rows + 2) * cols, outs), F32),
                VMEM((2, 1, chans), F32),
                VMEM((rows, cols, chans), BF16),
                VMEM((9, chans, outs), BF16),
                VMEM((chans, outs), BF16),
                dma((13,)),
            ],
            compiler_params=params(24),
            name="hidden",
        )(
            stats,
            up,
            in_hbm(latent),
            down,
            in_hbm(gain_in.reshape(1, -1)),
            in_hbm(shift_in.reshape(1, -1)),
            in_hbm(conv_in),
            in_hbm(skip_weight),
        )
    with jax.named_scope("exchange_mid"):
        stats_mid = lax.all_to_all(stats_mid, axis, 0, 0)

    with jax.named_scope("output"):
        return pl.pallas_call(
            functools.partial(
                output_kernel, float(4 * rows * cols * (outs // GROUPS) * peers), peers
            ),
            out_shape=whole((2 * rows, 2 * cols, outs), BF16),
            in_specs=[taken, taken, far, far, far, taken],
            out_specs=far,
            scratch_shapes=[
                VMEM((2 * rows + 2, cols, 4 * outs), BF16),
                VMEM((outs // LANES, 2 * cols, LANES), F32),
                VMEM((2 * rows, 2 * cols, outs), BF16),
                VMEM(conv_mid.shape, BF16),
                VMEM((2, 1, outs), F32),
                dma((2 * rows,)),
                dma((3,)),
            ],
            compiler_params=params(24),
            name="output",
        )(
            stats_mid,
            hidden,
            in_hbm(gain_mid.reshape(1, -1)),
            in_hbm(shift_mid.reshape(1, -1)),
            in_hbm(conv_mid),
            skipped,
        )


def solution(mesh):
    placed = (P(("groups", "rows"), None, None), P(), P(), P(), P(), P(), P(), P())
    return jax.shard_map(
        body,
        mesh=mesh,
        in_specs=placed,
        out_specs=P(("groups", "rows"), None, None),
        check_vma=False,
    )
```

```python
import functools

import jax
import jax.numpy as jnp
from jax import lax
from jax.experimental import pallas as pl
from jax.experimental.pallas import tpu as pltpu
from jax.sharding import PartitionSpec as P

GROUPS = 32
EPS = 1e-06
F32 = jnp.float32
BF16 = jnp.bfloat16
LANES = 128
GUARD = 8
SPLIT = 2
EARLY = 3
STEP = 16
VMEM = pltpu.VMEM


def vmem_spec():
    return pl.BlockSpec(memory_space=VMEM)


def in_hbm(values):
    return pltpu.with_memory_space_constraint(values, pltpu.HBM)


def params(limit_mib):
    return pltpu.CompilerParams(vmem_limit_bytes=limit_mib << 20)


def cost(flops, data):
    return pl.CostEstimate(flops=flops, bytes_accessed=data, transcendentals=0)


def stack_lanes(row):
    count = row.shape[1] // LANES
    return [row[:, i * LANES : (i + 1) * LANES] for i in range(count)]


def put_stats(out_ref, total, square):
    rows = stack_lanes(total) + stack_lanes(square)
    fill = 8 - len(rows)
    if fill:
        rows.append(jnp.zeros((fill, LANES), F32))
    tile = jnp.concatenate(rows, axis=0)
    out_ref[...] = jnp.broadcast_to(tile[None], out_ref.shape)


def get_affine(stats_ref, gain, shift, group_width, count):
    chans = gain.shape[1]
    half = chans // LANES
    total = jnp.sum(stats_ref[...], axis=0)
    left = lax.broadcasted_iota(jnp.int32, (LANES, LANES), 0) // group_width
    right = lax.broadcasted_iota(jnp.int32, (LANES, LANES), 1) // group_width
    same = (left == right).astype(F32)
    pooled = jnp.dot(total, same, preferred_element_type=F32, precision=lax.Precision.HIGHEST)
    scaled = pooled * (1.0 / count)
    center = jnp.concatenate([scaled[i : i + 1] for i in range(half)], axis=1)
    moment = jnp.concatenate([scaled[half + i : half + i + 1] for i in range(half)], axis=1)
    spread = jnp.maximum(moment - center * center, 0.0)
    scale = gain * lax.rsqrt(spread + EPS)
    return 0.5 * scale, 0.5 * (shift - center * scale)


def half_silu(values, scale, offset):
    halved = values * scale + offset
    return halved + halved * jnp.tanh(halved)


def shift_rows(values, step):
    size = values.shape[0]
    moved = pltpu.roll(values, step % size, 0)
    place = lax.broadcasted_iota(jnp.int32, (size, 1), 0)
    edge = 0 if step == 1 else size - 1
    return jnp.where(place == edge, 0.0, moved)


def stats_kernel(latent_ref, stats_ref, head_ref, tail_ref, held_ref, sems):
    rows = latent_ref.shape[0]
    copies = [
        pltpu.make_async_copy(latent_ref.at[row], held_ref.at[row], sems.at[row])
        for row in range(rows)
    ]
    for copy in copies:
        copy.start()
    total, square = 0.0, 0.0
    for row in range(rows):
        copies[row].wait()
        values = held_ref[row].astype(F32)
        total += jnp.sum(values, axis=0, keepdims=True)
        square += jnp.sum(values * values, axis=0, keepdims=True)
    put_stats(stats_ref, total, square)
    head_ref[0] = held_ref[0]
    tail_ref[0] = held_ref[rows - 1]


def fetch_all(pairs, sems):
    copies = [
        pltpu.make_async_copy(source, target, sems.at[index])
        for index, (source, target) in enumerate(pairs)
    ]
    for copy in copies:
        copy.start()
    return copies


def load_kernel(*refs):
    count = len(refs) // 2
    pairs = [
        (source.at[pl.ds(0, target.shape[0]), :], target)
        for source, target in zip(refs[:count], refs[count : 2 * count])
    ]
    for copy in fetch_all(pairs, refs[-1]):
        copy.wait()


def hidden_kernel(
    count,
    axis_count,
    stats_ref,
    up_ref,
    latent_ref,
    down_ref,
    gain_ref,
    shift_ref,
    weight_ref,
    rest_ref,
    hidden_ref,
    out_ref,
    middle_ref,
    act_ref,
    tap_ref,
    near_ref,
    late_ref,
    sems,
):
    rows, cols, chans = latent_ref.shape
    outs = weight_ref.shape[1]
    split = EARLY * chans
    fetched, fetched_late = fetch_all(
        [(latent_ref, near_ref), (rest_ref.at[pl.ds(split, (9 - EARLY) * chans), :], late_ref)],
        sems,
    )
    halves = outs // LANES
    pitch = cols + GUARD
    part = cols // SPLIT
    scale, offset = get_affine(stats_ref, gain_ref[...], shift_ref[...], chans // GROUPS, count)
    place = lax.axis_index("rows")
    total_rows = 2 * rows + 2
    sources = [[(row + tap - 2) // 2 + 1 for tap in range(3)] for row in range(total_rows)]
    zeros = jnp.zeros((GUARD, LANES), F32)
    for tap in range(9):
        if tap % 3 != 1:
            for row in range(rows + 3):
                for half in range(halves):
                    tap_ref[tap, half, row * pitch : row * pitch + GUARD, :] = zeros

    def fill(piece, wanted):
        span = slice(piece * part, (piece + 1) * part)
        for row in wanted:
            keep = None
            if row == 0:
                source, keep = up_ref[0, span], place > 0
            elif row == rows + 1:
                source, keep = down_ref[0, span], place < axis_count - 1
            else:
                source = near_ref[row - 1, span]
            act = half_silu(source.astype(F32), scale, offset)
            if keep is not None:
                act = act * keep.astype(F32)
            act_ref[row, span, :] = act.astype(BF16)

    def multiply(piece, taps):
        span = slice(piece * part, (piece + 1) * part)
        for tap in taps:
            if tap < EARLY:
                weight = weight_ref[tap * chans : (tap + 1) * chans, :]
            else:
                weight = late_ref[(tap - EARLY) * chans : (tap + 1 - EARLY) * chans, :]
            used = [source[tap // 3] for source in sources]
            first, last = min(used), max(used) + 1
            found = jnp.dot(
                act_ref[first:last, span, :].reshape(-1, chans),
                weight,
                preferred_element_type=F32,
            )
            for row in range(first, last):
                start = row * pitch + GUARD + piece * part
                for half in range(halves):
                    tap_ref[tap, half, start : start + part, :] = found[
                        (row - first) * part : (row - first + 1) * part,
                        half * LANES : (half + 1) * LANES,
                    ]

    totals = [jnp.zeros((8, LANES), F32)] * halves
    squares = [jnp.zeros((8, LANES), F32)] * halves

    def combine(chunk):
        for half in range(halves):
            sums = {}
            for row, tap in sorted({(s[a], a) for s in sources for a in range(3)}):
                start = row * pitch + GUARD + chunk * STEP

                def get(b, move):
                    return tap_ref[3 * tap + b, half, start + move : start + move + STEP, :]

                left, center, right = get(0, 0), get(1, 0), get(2, 0)
                sums[row, tap] = (
                    get(0, -1) + (center + right),
                    (left + center) + get(2, 1),
                )
            for row in range(total_rows):
                for phase in range(2):
                    pieces = [sums[sources[row][a], a][phase] for a in range(3)]
                    found = (pieces[0] + pieces[1] + pieces[2]).astype(BF16)
                    hidden_ref[
                        row,
                        phase,
                        chunk * STEP : (chunk + 1) * STEP,
                        half * LANES : (half + 1) * LANES,
                    ] = found
                    if 0 < row < total_rows - 1:
                        wide = found.astype(F32)
                        upper, lower = wide[:8], wide[8:]
                        totals[half] = totals[half] + (upper + lower)
                        squares[half] = squares[half] + (upper * upper + lower * lower)

    chunks = cols // STEP
    ready = [(piece + 1) * part // STEP - 1 for piece in range(SPLIT)]
    ready[-1] = chunks
    for piece in range(SPLIT):
        fill(piece, (0, rows + 1))
    fetched.wait()
    for piece in range(SPLIT):
        fill(piece, range(1, rows + 1))
        multiply(piece, range(EARLY))
    middle_ref[...] = act_ref[1 : rows + 1].reshape(-1, chans)
    fetched_late.wait()
    for piece in range(SPLIT):
        multiply(piece, range(EARLY, 9))
    done = 0
    for piece in range(SPLIT):
        for chunk in range(done, ready[piece]):
            combine(chunk)
        done = ready[piece]
    put_stats(
        out_ref,
        jnp.concatenate([jnp.sum(t, axis=0, keepdims=True) for t in totals], axis=1),
        jnp.concatenate([jnp.sum(t, axis=0, keepdims=True) for t in squares], axis=1),
    )


def skip_kernel(
    middle_ref,
    skip_ref,
    gain_ref,
    shift_ref,
    skipped_ref,
    gain_out_ref,
    shift_out_ref,
    held_ref,
    sems,
):
    copies = fetch_all(
        [
            (skip_ref, held_ref),
            (gain_ref, gain_out_ref),
            (shift_ref, shift_out_ref),
        ],
        sems,
    )
    for copy in copies:
        copy.wait()
    skipped_ref[...] = jnp.dot(middle_ref[...], held_ref[...], preferred_element_type=F32)


def output_kernel(
    count,
    axis_count,
    stats_ref,
    hidden_ref,
    gain_ref,
    shift_ref,
    weight_ref,
    skipped_ref,
    out_ref,
    mid_ref,
    mixed_ref,
    done_ref,
    held_ref,
    sems,
    held_sem,
):
    fetched = pltpu.make_async_copy(weight_ref, held_ref, held_sem)
    fetched.start()
    total_rows, _, cols, chans = hidden_ref.shape
    rows = total_rows - 2
    scale, offset = get_affine(stats_ref, gain_ref[...], shift_ref[...], chans // GROUPS, count)
    place = lax.axis_index("rows")

    def fill(row):
        pair = []
        keep = None
        if row == 0:
            keep = place > 0
        elif row == rows + 1:
            keep = place < axis_count - 1
        for phase in range(2):
            value = half_silu(hidden_ref[row, phase].astype(F32), scale, offset)
            if keep is not None:
                value = value * keep.astype(F32)
            pair.append(value)
        even, odd = pair
        mid_ref[row, :, 0:chans] = shift_rows(odd, 1).astype(BF16)
        mid_ref[row, :, chans : 2 * chans] = even.astype(BF16)
        mid_ref[row, :, 2 * chans : 3 * chans] = odd.astype(BF16)
        mid_ref[row, :, 3 * chans :] = shift_rows(even, -1).astype(BF16)

    def multiply(low):
        lhs = jnp.concatenate(
            [
                jnp.concatenate(
                    [
                        mid_ref[2 * low + tap : 2 * low + tap + 2, :, window].reshape(
                            -1, 3 * chans
                        )
                        for tap in range(3)
                    ],
                    axis=1,
                )
                for window in (slice(0, 3 * chans), slice(chans, 4 * chans))
            ],
            axis=0,
        )
        return jnp.dot(lhs, held_ref[...], preferred_element_type=F32)

    def finish(low, found):
        base = skipped_ref[low * cols : (low + 1) * cols, :]
        for side in range(2):
            row = 2 * low + side
            for phase in range(2):
                start = (2 * phase + side) * cols
                value = base + found[start : start + cols]
                for half in range(chans // LANES):
                    mixed_ref[row, half, pl.ds(phase, cols, stride=2), :] = value[
                        :, half * LANES : (half + 1) * LANES
                    ]
            for half in range(chans // LANES):
                done_ref[row, :, half * LANES : (half + 1) * LANES] = mixed_ref[row, half].astype(
                    BF16
                )

    found = []
    filled = 0
    for low in range(rows // 2):
        for row in range(filled, 2 * low + 4):
            fill(row)
        filled = 2 * low + 4
        if low == 0:
            fetched.wait()
        found.append(multiply(low))
    copies = []
    for low in range(rows // 2):
        finish(low, found[low])
        for row in (2 * low, 2 * low + 1):
            copies.append(pltpu.make_async_copy(done_ref.at[row], out_ref.at[row], sems.at[row]))
            copies[-1].start()
    for copy in copies:
        copy.wait()


def body(latent, gain_in, shift_in, conv_in, gain_mid, shift_mid, conv_mid, skip_weight):
    axis = "rows"
    peers = lax.axis_size(axis)
    rows, cols, chans = latent.shape
    outs = conv_in.shape[1]
    ends = peers - 1
    taken = vmem_spec()
    far = pl.BlockSpec(memory_space=pltpu.HBM)
    dma = pltpu.SemaphoreType.DMA
    whole = jax.ShapeDtypeStruct

    with jax.named_scope("stats"):
        stats, head, tail = pl.pallas_call(
            stats_kernel,
            out_shape=(
                whole((peers, 8, LANES), F32),
                whole((1, cols, chans), BF16),
                whole((1, cols, chans), BF16),
            ),
            in_specs=[far],
            out_specs=(taken,) * 3,
            scratch_shapes=[VMEM(latent.shape, BF16), dma((rows,))],
            compiler_params=params(16),
            name="stats",
        )(in_hbm(latent))
    with jax.named_scope("exchange_in"):
        stats = lax.all_to_all(stats, axis, 0, 0)
    with jax.named_scope("halo"):
        up = lax.ppermute(tail, axis, [(i, i + 1) for i in range(ends)])
        down = lax.ppermute(head, axis, [(i + 1, i) for i in range(ends)])

    with jax.named_scope("load"):
        ready = [gain_in.reshape(1, -1), shift_in.reshape(1, -1), conv_in]
        ready = pl.pallas_call(
            load_kernel,
            out_shape=[
                VMEM((1, chans), F32),
                VMEM((1, chans), F32),
                VMEM((EARLY * chans, outs), BF16),
            ],
            in_specs=[far] * 3,
            out_specs=[taken] * 3,
            scratch_shapes=[dma((3,))],
            compiler_params=params(4),
            cost_estimate=cost(4 << 20, 8 << 20),
            name="load",
        )(*map(in_hbm, ready))
        near_gain, near_shift, near_conv = ready

    with jax.named_scope("hidden"):
        hidden, stats_mid, middle = pl.pallas_call(
            functools.partial(
                hidden_kernel, float(rows * cols * (chans // GROUPS) * peers), peers
            ),
            out_shape=(
                whole((2 * rows + 2, 2, cols, outs), BF16),
                whole((peers, 8, LANES), F32),
                whole((rows * cols, chans), BF16),
            ),
            in_specs=[taken, taken, far, taken, taken, taken, taken, far],
            out_specs=(taken,) * 3,
            scratch_shapes=[
                VMEM((rows + 2, cols, chans), BF16),
                VMEM((9, outs // LANES, (rows + 2) * (cols + GUARD) + GUARD, LANES), F32),
                VMEM(latent.shape, BF16),
                VMEM(((9 - EARLY) * chans, outs), BF16),
                dma((2,)),
            ],
            compiler_params=params(24),
            name="hidden",
        )(stats, up, in_hbm(latent), down, near_gain, near_shift, near_conv, in_hbm(conv_in))
    with jax.named_scope("exchange_mid"):
        stats_mid = lax.all_to_all(stats_mid, axis, 0, 0)

    with jax.named_scope("skip"):
        skipped, near_gain, near_shift = pl.pallas_call(
            skip_kernel,
            out_shape=[
                VMEM((rows * cols, outs), F32),
                VMEM((1, outs), F32),
                VMEM((1, outs), F32),
            ],
            in_specs=[taken] + [far] * 3,
            out_specs=[taken] * 3,
            scratch_shapes=[VMEM((chans, outs), BF16), dma((3,))],
            compiler_params=params(4),
            cost_estimate=cost(200 << 20, 8 << 20),
            name="skip",
        )(
            middle,
            in_hbm(skip_weight),
            in_hbm(gain_mid.reshape(1, -1)),
            in_hbm(shift_mid.reshape(1, -1)),
        )

    with jax.named_scope("output"):
        return pl.pallas_call(
            functools.partial(
                output_kernel, float(4 * rows * cols * (outs // GROUPS) * peers), peers
            ),
            out_shape=whole((2 * rows, 2 * cols, outs), BF16),
            in_specs=[taken] * 4 + [far, taken],
            out_specs=far,
            scratch_shapes=[
                VMEM((2 * rows + 2, cols, 4 * outs), BF16),
                VMEM((2 * rows, outs // LANES, 2 * cols, LANES), F32),
                VMEM((2 * rows, 2 * cols, outs), BF16),
                VMEM(conv_mid.shape, BF16),
                dma((2 * rows,)),
                dma,
            ],
            compiler_params=params(24),
            name="output",
        )(stats_mid, hidden, near_gain, near_shift, in_hbm(conv_mid), skipped)


def solution(mesh):
    placed = (P(("groups", "rows"), None, None), P(), P(), P(), P(), P(), P(), P())
    return jax.shard_map(
        body,
        mesh=mesh,
        in_specs=placed,
        out_specs=P(("groups", "rows"), None, None),
        check_vma=False,
    )
```

```python
import functools

import jax
import jax.numpy as jnp
from jax import lax
from jax.experimental import pallas as pl
from jax.experimental.pallas import tpu as pltpu
from jax.sharding import PartitionSpec as P


GROUPS = 32
EPS = 1e-06
F32 = jnp.float32
BF16 = jnp.bfloat16
LANES = 128
GUARD = 8
SPLIT = 2
EARLY = 1
STEP = 16
VMEM = pltpu.VMEM


def vmem_spec():
    return pl.BlockSpec(memory_space=VMEM)


def in_hbm(values):
    return pltpu.with_memory_space_constraint(values, pltpu.HBM)


def params(limit_mib):
    return pltpu.CompilerParams(vmem_limit_bytes=limit_mib << 20)


def cost(flops, data):
    return pl.CostEstimate(flops=flops, bytes_accessed=data, transcendentals=0)


def stack_lanes(row):
    count = row.shape[1] // LANES
    return [row[:, i * LANES : (i + 1) * LANES] for i in range(count)]


def put_stats(out_ref, total, square):
    rows = stack_lanes(total) + stack_lanes(square)
    fill = 8 - len(rows)
    if fill:
        rows.append(jnp.zeros((fill, LANES), F32))
    tile = jnp.concatenate(rows, axis=0)
    out_ref[...] = jnp.broadcast_to(tile[None], out_ref.shape)


def get_affine(stats_ref, gain, shift, group_width, count):
    chans = gain.shape[1]
    half = chans // LANES
    total = jnp.sum(stats_ref[...], axis=0)
    left = lax.broadcasted_iota(jnp.int32, (LANES, LANES), 0) // group_width
    right = lax.broadcasted_iota(jnp.int32, (LANES, LANES), 1) // group_width
    same = (left == right).astype(F32)
    pooled = jnp.dot(total, same, preferred_element_type=F32, precision=lax.Precision.HIGHEST)
    scaled = pooled * (1.0 / count)
    center = jnp.concatenate([scaled[i : i + 1] for i in range(half)], axis=1)
    moment = jnp.concatenate([scaled[half + i : half + i + 1] for i in range(half)], axis=1)
    spread = jnp.maximum(moment - center * center, 0.0)
    scale = gain * lax.rsqrt(spread + EPS)
    return 0.5 * scale, 0.5 * (shift - center * scale)


def half_silu(values, scale, offset):
    halved = values * scale + offset
    return halved + halved * jnp.tanh(halved)


def shift_rows(values, step):
    size = values.shape[0]
    moved = pltpu.roll(values, step % size, 0)
    place = lax.broadcasted_iota(jnp.int32, (size, 1), 0)
    edge = 0 if step == 1 else size - 1
    return jnp.where(place == edge, 0.0, moved)


def stats_kernel(latent_ref, stats_ref, near_ref, far_ref, held_ref, sems):
    rows = latent_ref.shape[0]
    copies = [
        pltpu.make_async_copy(latent_ref.at[row], held_ref.at[row], sems.at[row])
        for row in range(rows)
    ]
    for copy in copies:
        copy.start()
    total, square = 0.0, 0.0
    for row in range(rows):
        copies[row].wait()
        values = held_ref[row].astype(F32)
        total += jnp.sum(values, axis=0, keepdims=True)
        square += jnp.sum(values * values, axis=0, keepdims=True)
    put_stats(stats_ref, total, square)
    odd = lax.rem(lax.axis_index("rows"), 2)
    near_ref[0] = held_ref[(1 - odd) * (rows - 1)]
    far_ref[0] = held_ref[odd * (rows - 1)]


def fetch_all(pairs, sems):
    copies = [
        pltpu.make_async_copy(source, target, sems.at[index])
        for index, (source, target) in enumerate(pairs)
    ]
    for copy in copies:
        copy.start()
    return copies


def load_kernel(*refs):
    count = len(refs) // 2
    pairs = [
        (source.at[pl.ds(0, target.shape[0])], target)
        for source, target in zip(refs[:count], refs[count : 2 * count])
    ]
    for copy in fetch_all(pairs, refs[-1]):
        copy.wait()


def hidden_kernel(
    count,
    axis_count,
    stats_ref,
    near_row_ref,
    far_row_ref,
    latent_ref,
    gain_ref,
    shift_ref,
    weight_ref,
    rest_ref,
    skip_ref,
    hidden_ref,
    out_ref,
    skipped_ref,
    act_ref,
    tap_ref,
    late_ref,
    skips_ref,
    sems,
):
    rows, cols, chans = latent_ref.shape
    outs = weight_ref.shape[1]
    split = EARLY * chans
    fetched = fetch_all(
        [(rest_ref.at[pl.ds(split, (9 - EARLY) * chans), :], late_ref), (skip_ref, skips_ref)],
        sems,
    )
    halves = outs // LANES
    pitch = cols + GUARD
    part = cols // SPLIT
    scale, offset = get_affine(stats_ref, gain_ref[...], shift_ref[...], chans // GROUPS, count)
    place = lax.axis_index("rows")
    odd = lax.rem(place, 2) == 1
    total_rows = 2 * rows + 2
    sources = [[(row + tap - 2) // 2 + 1 for tap in range(3)] for row in range(total_rows)]
    zeros = jnp.zeros((GUARD, LANES), F32)
    for tap in range(9):
        if tap % 3 != 1:
            for row in range(rows + 3):
                for half in range(halves):
                    tap_ref[tap, half, row * pitch : row * pitch + GUARD, :] = zeros

    def fill(piece, wanted):
        span = slice(piece * part, (piece + 1) * part)
        for row in wanted:
            keep = None
            if row == 0:
                keep = place > 0
                source = jnp.where(odd, near_row_ref[0, span].astype(F32), far_row_ref[0, span].astype(F32))
            elif row == rows + 1:
                keep = place < axis_count - 1
                source = jnp.where(odd, far_row_ref[0, span].astype(F32), near_row_ref[0, span].astype(F32))
            else:
                source = latent_ref[row - 1, span].astype(F32)
            act = half_silu(source, scale, offset)
            if keep is not None:
                act = act * keep.astype(F32)
            act_ref[row, span, :] = act.astype(BF16)

    def multiply(piece, taps):
        span = slice(piece * part, (piece + 1) * part)
        for tap in taps:
            if tap < EARLY:
                weight = weight_ref[tap * chans : (tap + 1) * chans, :]
            else:
                weight = late_ref[(tap - EARLY) * chans : (tap + 1 - EARLY) * chans, :]
            used = [source[tap // 3] for source in sources]
            first, last = min(used), max(used) + 1
            found = jnp.dot(
                act_ref[first:last, span, :].reshape(-1, chans),
                weight,
                preferred_element_type=F32,
            )
            for row in range(first, last):
                start = row * pitch + GUARD + piece * part
                for half in range(halves):
                    tap_ref[tap, half, start : start + part, :] = found[
                        (row - first) * part : (row - first + 1) * part,
                        half * LANES : (half + 1) * LANES,
                    ]

    totals = [jnp.zeros((8, LANES), F32)] * halves
    squares = [jnp.zeros((8, LANES), F32)] * halves

    def combine(chunk):
        for half in range(halves):
            sums = {}
            for row, tap in sorted({(s[a], a) for s in sources for a in range(3)}):
                start = row * pitch + GUARD + chunk * STEP

                def get(b, move):
                    return tap_ref[3 * tap + b, half, start + move : start + move + STEP, :]

                left, center, right = get(0, 0), get(1, 0), get(2, 0)
                sums[row, tap] = (
                    get(0, -1) + (center + right),
                    (left + center) + get(2, 1),
                )
            for row in range(total_rows):
                for phase in range(2):
                    pieces = [sums[sources[row][a], a][phase] for a in range(3)]
                    found = (pieces[0] + pieces[1] + pieces[2]).astype(BF16)
                    hidden_ref[
                        row,
                        phase,
                        chunk * STEP : (chunk + 1) * STEP,
                        half * LANES : (half + 1) * LANES,
                    ] = found
                    if 0 < row < total_rows - 1:
                        wide = found.astype(F32)
                        upper, lower = wide[:8], wide[8:]
                        totals[half] = totals[half] + (upper + lower)
                        squares[half] = squares[half] + (upper * upper + lower * lower)

    chunks = cols // STEP
    ready = [(piece + 1) * part // STEP - 1 for piece in range(SPLIT)]
    ready[-1] = chunks
    for piece in range(SPLIT):
        fill(piece, range(rows + 2))
        multiply(piece, range(EARLY))
    for copy in fetched:
        copy.wait()
    for piece in range(SPLIT):
        multiply(piece, range(EARLY, 9))
    skipped_ref[...] = jnp.dot(
        act_ref[1 : rows + 1].reshape(-1, chans), skips_ref[...], preferred_element_type=F32
    )
    done = 0
    for piece in range(SPLIT):
        for chunk in range(done, ready[piece]):
            combine(chunk)
        done = ready[piece]
    put_stats(
        out_ref,
        jnp.concatenate([jnp.sum(t, axis=0, keepdims=True) for t in totals], axis=1),
        jnp.concatenate([jnp.sum(t, axis=0, keepdims=True) for t in squares], axis=1),
    )


def output_kernel(
    count,
    axis_count,
    stats_ref,
    hidden_ref,
    gain_ref,
    shift_ref,
    weight_ref,
    skipped_ref,
    out_ref,
    mid_ref,
    mixed_ref,
    done_ref,
    sems,
):
    total_rows, _, cols, chans = hidden_ref.shape
    rows = total_rows - 2
    scale, offset = get_affine(stats_ref, gain_ref[...], shift_ref[...], chans // GROUPS, count)
    place = lax.axis_index("rows")

    def fill(row):
        pair = []
        keep = None
        if row == 0:
            keep = place > 0
        elif row == rows + 1:
            keep = place < axis_count - 1
        for phase in range(2):
            value = half_silu(hidden_ref[row, phase].astype(F32), scale, offset)
            if keep is not None:
                value = value * keep.astype(F32)
            pair.append(value)
        even, odd = pair
        mid_ref[row, :, 0:chans] = shift_rows(odd, 1).astype(BF16)
        mid_ref[row, :, chans : 2 * chans] = even.astype(BF16)
        mid_ref[row, :, 2 * chans : 3 * chans] = odd.astype(BF16)
        mid_ref[row, :, 3 * chans :] = shift_rows(even, -1).astype(BF16)

    def multiply(low):
        lhs = jnp.concatenate(
            [
                jnp.concatenate(
                    [
                        mid_ref[2 * low + tap : 2 * low + tap + 2, :, window].reshape(
                            -1, 3 * chans
                        )
                        for tap in range(3)
                    ],
                    axis=1,
                )
                for window in (slice(0, 3 * chans), slice(chans, 4 * chans))
            ],
            axis=0,
        )
        return jnp.dot(lhs, weight_ref[...], preferred_element_type=F32)

    def finish(low, found):
        base = skipped_ref[low * cols : (low + 1) * cols, :]
        for side in range(2):
            row = 2 * low + side
            for phase in range(2):
                start = (2 * phase + side) * cols
                value = base + found[start : start + cols]
                for half in range(chans // LANES):
                    mixed_ref[row, half, pl.ds(phase, cols, stride=2), :] = value[
                        :, half * LANES : (half + 1) * LANES
                    ]
            for half in range(chans // LANES):
                done_ref[row, :, half * LANES : (half + 1) * LANES] = mixed_ref[row, half].astype(
                    BF16
                )

    found = []
    filled = 0
    for low in range(rows // 2):
        for row in range(filled, 2 * low + 4):
            fill(row)
        filled = 2 * low + 4
        found.append(multiply(low))
    copies = []
    for low in range(rows // 2):
        finish(low, found[low])
        for row in (2 * low, 2 * low + 1):
            copies.append(pltpu.make_async_copy(done_ref.at[row], out_ref.at[row], sems.at[row]))
            copies[-1].start()
    for copy in copies:
        copy.wait()


def body(latent, gain_in, shift_in, conv_in, gain_mid, shift_mid, conv_mid, skip_weight):
    axis = "rows"
    peers = lax.axis_size(axis)
    rows, cols, chans = latent.shape
    outs = conv_in.shape[1]
    ends = peers - 1
    taken = vmem_spec()
    far = pl.BlockSpec(memory_space=pltpu.HBM)
    dma = pltpu.SemaphoreType.DMA
    whole = jax.ShapeDtypeStruct

    stats, near_row, far_row = pl.pallas_call(
        stats_kernel,
        out_shape=(
            whole((peers, 8, LANES), F32),
            whole((1, cols, chans), BF16),
            whole((1, cols, chans), BF16),
        ),
        in_specs=[far],
        out_specs=(taken,) * 3,
        scratch_shapes=[VMEM(latent.shape, BF16), dma((rows,))],
        compiler_params=params(16),
        name="stats",
    )(in_hbm(latent))
    inner = range(1, ends)
    far_row = lax.ppermute(far_row, axis, [(i, i + 1 if i % 2 else i - 1) for i in inner])
    stats = lax.all_to_all(stats, axis, 0, 0)
    near_row = lax.ppermute(near_row, axis, [(i, i ^ 1) for i in range(peers)])

    ready = [latent, gain_in.reshape(1, -1), shift_in.reshape(1, -1), conv_in]
    ready = pl.pallas_call(
        load_kernel,
        out_shape=[
            VMEM(latent.shape, BF16),
            VMEM((1, chans), F32),
            VMEM((1, chans), F32),
            VMEM((EARLY * chans, outs), BF16),
        ],
        in_specs=[far] * 4,
        out_specs=[taken] * 4,
        scratch_shapes=[dma((4,))],
        compiler_params=params(4),
        cost_estimate=cost(4 << 20, 8 << 20),
        name="load",
    )(*map(in_hbm, ready))
    near_latent, near_gain, near_shift, near_conv = ready

    hidden, stats_mid, skipped = pl.pallas_call(
        functools.partial(
            hidden_kernel, float(rows * cols * (chans // GROUPS) * peers), peers
        ),
        out_shape=(
            whole((2 * rows + 2, 2, cols, outs), BF16),
            whole((peers, 8, LANES), F32),
            whole((rows * cols, outs), F32),
        ),
        in_specs=[taken] * 7 + [far] * 2,
        out_specs=(taken,) * 3,
        scratch_shapes=[
            VMEM((rows + 2, cols, chans), BF16),
            VMEM((9, outs // LANES, (rows + 2) * (cols + GUARD) + GUARD, LANES), F32),
            VMEM(((9 - EARLY) * chans, outs), BF16),
            VMEM((chans, outs), BF16),
            dma((2,)),
        ],
        compiler_params=params(24),
        name="hidden",
    )(
        stats,
        near_row,
        far_row,
        near_latent,
        near_gain,
        near_shift,
        near_conv,
        in_hbm(conv_in),
        in_hbm(skip_weight),
    )
    stats_mid = lax.all_to_all(stats_mid, axis, 0, 0)

    ready = [gain_mid.reshape(1, -1), shift_mid.reshape(1, -1), conv_mid]
    near_gain, near_shift, near_mid = pl.pallas_call(
        load_kernel,
        out_shape=[VMEM(part.shape, part.dtype) for part in ready],
        in_specs=[far] * 3,
        out_specs=[taken] * 3,
        scratch_shapes=[dma((3,))],
        compiler_params=params(4),
        cost_estimate=cost(4 << 20, 8 << 20),
        name="load_mid",
    )(*map(in_hbm, ready))

    return pl.pallas_call(
        functools.partial(output_kernel, float(4 * rows * cols * (outs // GROUPS) * peers), peers),
        out_shape=whole((2 * rows, 2 * cols, outs), BF16),
        in_specs=[taken] * 6,
        out_specs=far,
        scratch_shapes=[
            VMEM((2 * rows + 2, cols, 4 * outs), BF16),
            VMEM((2 * rows, outs // LANES, 2 * cols, LANES), F32),
            VMEM((2 * rows, 2 * cols, outs), BF16),
            dma((2 * rows,)),
        ],
        compiler_params=params(24),
        name="output",
    )(stats_mid, hidden, near_gain, near_shift, near_mid, skipped)


def solution(mesh):
    placed = (P(("groups", "rows"), None, None), P(), P(), P(), P(), P(), P(), P())
    return jax.shard_map(
        body,
        mesh=mesh,
        in_specs=placed,
        out_specs=P(("groups", "rows"), None, None),
        check_vma=False,
    )
```

```python
import functools

import jax
import jax.numpy as jnp
from jax import lax
from jax.experimental import pallas as pl
from jax.experimental.pallas import tpu as pltpu
from jax.sharding import PartitionSpec as P


GROUPS = 32
EPS = 1e-06
F32 = jnp.float32
BF16 = jnp.bfloat16
LANES = 128
GUARD = 8
SPLIT = 2
STEP = 16
VMEM = pltpu.VMEM


def vmem_spec():
    return pl.BlockSpec(memory_space=VMEM)


def in_hbm(values):
    return pltpu.with_memory_space_constraint(values, pltpu.HBM)


def params(limit_mib):
    return pltpu.CompilerParams(vmem_limit_bytes=limit_mib << 20)


def cost(flops, data):
    return pl.CostEstimate(flops=flops, bytes_accessed=data, transcendentals=0)


def stack_lanes(row):
    count = row.shape[1] // LANES
    return [row[:, i * LANES : (i + 1) * LANES] for i in range(count)]


def put_stats(out_ref, total, square):
    rows = stack_lanes(total) + stack_lanes(square)
    fill = 8 - len(rows)
    if fill:
        rows.append(jnp.zeros((fill, LANES), F32))
    tile = jnp.concatenate(rows, axis=0)
    out_ref[...] = jnp.broadcast_to(tile[None], out_ref.shape)


def get_affine(stats_ref, gain, shift, group_width, count):
    chans = gain.shape[1]
    half = chans // LANES
    total = jnp.sum(stats_ref[...], axis=0)
    left = lax.broadcasted_iota(jnp.int32, (LANES, LANES), 0) // group_width
    right = lax.broadcasted_iota(jnp.int32, (LANES, LANES), 1) // group_width
    same = (left == right).astype(F32)
    pooled = jnp.dot(total, same, preferred_element_type=F32, precision=lax.Precision.HIGHEST)
    scaled = pooled * (1.0 / count)
    center = jnp.concatenate([scaled[i : i + 1] for i in range(half)], axis=1)
    moment = jnp.concatenate([scaled[half + i : half + i + 1] for i in range(half)], axis=1)
    spread = jnp.maximum(moment - center * center, 0.0)
    scale = gain * lax.rsqrt(spread + EPS)
    return 0.5 * scale, 0.5 * (shift - center * scale)


def half_silu(values, scale, offset):
    halved = values * scale + offset
    return halved + halved * jnp.tanh(halved)


def shift_rows(values, step):
    size = values.shape[0]
    moved = pltpu.roll(values, step % size, 0)
    place = lax.broadcasted_iota(jnp.int32, (size, 1), 0)
    edge = 0 if step == 1 else size - 1
    return jnp.where(place == edge, 0.0, moved)


def stats_kernel(latent_ref, stats_ref, near_ref, far_ref, held_ref, sems):
    rows = latent_ref.shape[0]
    copies = [
        pltpu.make_async_copy(latent_ref.at[row], held_ref.at[row], sems.at[row])
        for row in range(rows)
    ]
    for copy in copies:
        copy.start()
    total, square = 0.0, 0.0
    for row in range(rows):
        copies[row].wait()
        values = held_ref[row].astype(F32)
        total += jnp.sum(values, axis=0, keepdims=True)
        square += jnp.sum(values * values, axis=0, keepdims=True)
    put_stats(stats_ref, total, square)
    odd = lax.rem(lax.axis_index("rows"), 2)
    near_ref[0] = held_ref[(1 - odd) * (rows - 1)]
    far_ref[0] = held_ref[odd * (rows - 1)]


def fetch_all(pairs, sems):
    copies = [
        pltpu.make_async_copy(source, target, sems.at[index])
        for index, (source, target) in enumerate(pairs)
    ]
    for copy in copies:
        copy.start()
    return copies


def load_kernel(*refs):
    count = len(refs) // 2
    pairs = [
        (source.at[pl.ds(0, target.shape[0])], target)
        for source, target in zip(refs[:count], refs[count : 2 * count])
    ]
    for copy in fetch_all(pairs, refs[-1]):
        copy.wait()


def hidden_kernel(
    count,
    axis_count,
    stats_ref,
    near_row_ref,
    far_row_ref,
    latent_ref,
    gain_ref,
    shift_ref,
    weight_ref,
    hidden_ref,
    out_ref,
    affine_ref,
    act_ref,
    tap_ref,
):
    rows, cols, chans = latent_ref.shape
    outs = weight_ref.shape[1]
    halves = outs // LANES
    pitch = cols + GUARD
    part = cols // SPLIT
    scale, offset = get_affine(stats_ref, gain_ref[...], shift_ref[...], chans // GROUPS, count)
    affine_ref[0] = scale
    affine_ref[1] = offset
    place = lax.axis_index("rows")
    odd = lax.rem(place, 2) == 1
    total_rows = 2 * rows + 2
    sources = [[(row + tap - 2) // 2 + 1 for tap in range(3)] for row in range(total_rows)]
    zeros = jnp.zeros((GUARD, LANES), F32)
    for tap in range(9):
        if tap % 3 != 1:
            for row in range(rows + 3):
                for half in range(halves):
                    tap_ref[tap, half, row * pitch : row * pitch + GUARD, :] = zeros

    def fill(piece, wanted):
        span = slice(piece * part, (piece + 1) * part)
        for row in wanted:
            keep = None
            if row == 0:
                keep = place > 0
                source = jnp.where(odd, near_row_ref[0, span].astype(F32), far_row_ref[0, span].astype(F32))
            elif row == rows + 1:
                keep = place < axis_count - 1
                source = jnp.where(odd, far_row_ref[0, span].astype(F32), near_row_ref[0, span].astype(F32))
            else:
                source = latent_ref[row - 1, span].astype(F32)
            act = half_silu(source, scale, offset)
            if keep is not None:
                act = act * keep.astype(F32)
            act_ref[row, span, :] = act.astype(BF16)

    def multiply(piece, taps):
        span = slice(piece * part, (piece + 1) * part)
        for tap in taps:
            weight = weight_ref[tap * chans : (tap + 1) * chans, :]
            used = [source[tap // 3] for source in sources]
            first, last = min(used), max(used) + 1
            found = jnp.dot(
                act_ref[first:last, span, :].reshape(-1, chans),
                weight,
                preferred_element_type=F32,
            )
            for row in range(first, last):
                start = row * pitch + GUARD + piece * part
                for half in range(halves):
                    tap_ref[tap, half, start : start + part, :] = found[
                        (row - first) * part : (row - first + 1) * part,
                        half * LANES : (half + 1) * LANES,
                    ]

    totals = [jnp.zeros((8, LANES), F32)] * halves
    squares = [jnp.zeros((8, LANES), F32)] * halves

    def combine(chunk):
        for half in range(halves):
            sums = {}
            for row, tap in sorted({(s[a], a) for s in sources for a in range(3)}):
                start = row * pitch + GUARD + chunk * STEP

                def get(b, move):
                    return tap_ref[3 * tap + b, half, start + move : start + move + STEP, :]

                left, center, right = get(0, 0), get(1, 0), get(2, 0)
                sums[row, tap] = (
                    get(0, -1) + (center + right),
                    (left + center) + get(2, 1),
                )
            for row in range(total_rows):
                for phase in range(2):
                    pieces = [sums[sources[row][a], a][phase] for a in range(3)]
                    found = (pieces[0] + pieces[1] + pieces[2]).astype(BF16)
                    hidden_ref[
                        row,
                        phase,
                        chunk * STEP : (chunk + 1) * STEP,
                        half * LANES : (half + 1) * LANES,
                    ] = found
                    if 0 < row < total_rows - 1:
                        wide = found.astype(F32)
                        upper, lower = wide[:8], wide[8:]
                        totals[half] = totals[half] + (upper + lower)
                        squares[half] = squares[half] + (upper * upper + lower * lower)

    chunks = cols // STEP
    ready = [(piece + 1) * part // STEP - 1 for piece in range(SPLIT)]
    ready[-1] = chunks
    for piece in range(SPLIT):
        fill(piece, range(rows + 2))
        multiply(piece, range(9))
    done = 0
    for piece in range(SPLIT):
        for chunk in range(done, ready[piece]):
            combine(chunk)
        done = ready[piece]
    put_stats(
        out_ref,
        jnp.concatenate([jnp.sum(t, axis=0, keepdims=True) for t in totals], axis=1),
        jnp.concatenate([jnp.sum(t, axis=0, keepdims=True) for t in squares], axis=1),
    )


def skip_kernel(
    affine_ref,
    gain_ref,
    shift_ref,
    weight_ref,
    latent_ref,
    skip_ref,
    gain_out_ref,
    shift_out_ref,
    weight_out_ref,
    skipped_ref,
    near_ref,
    held_ref,
    sems,
):
    copies = fetch_all(
        [
            (latent_ref, near_ref),
            (skip_ref, held_ref),
            (gain_ref, gain_out_ref),
            (shift_ref, shift_out_ref),
            (weight_ref, weight_out_ref),
        ],
        sems,
    )
    copies[0].wait()
    copies[1].wait()
    values = near_ref[...].astype(F32).reshape(-1, near_ref.shape[2])
    act = half_silu(values, affine_ref[0], affine_ref[1]).astype(BF16)
    skipped_ref[...] = jnp.dot(act, held_ref[...], preferred_element_type=F32)
    for copy in copies[2:]:
        copy.wait()


def output_kernel(
    count,
    axis_count,
    stats_ref,
    hidden_ref,
    gain_ref,
    shift_ref,
    weight_ref,
    skipped_ref,
    out_ref,
    mid_ref,
    mixed_ref,
    done_ref,
    sems,
):
    total_rows, _, cols, chans = hidden_ref.shape
    rows = total_rows - 2
    scale, offset = get_affine(stats_ref, gain_ref[...], shift_ref[...], chans // GROUPS, count)
    place = lax.axis_index("rows")

    def fill(row):
        pair = []
        keep = None
        if row == 0:
            keep = place > 0
        elif row == rows + 1:
            keep = place < axis_count - 1
        for phase in range(2):
            value = half_silu(hidden_ref[row, phase].astype(F32), scale, offset)
            if keep is not None:
                value = value * keep.astype(F32)
            pair.append(value)
        even, odd = pair
        mid_ref[row, :, 0:chans] = shift_rows(odd, 1).astype(BF16)
        mid_ref[row, :, chans : 2 * chans] = even.astype(BF16)
        mid_ref[row, :, 2 * chans : 3 * chans] = odd.astype(BF16)
        mid_ref[row, :, 3 * chans :] = shift_rows(even, -1).astype(BF16)

    def multiply(low):
        lhs = jnp.concatenate(
            [
                jnp.concatenate(
                    [
                        mid_ref[2 * low + tap : 2 * low + tap + 2, :, window].reshape(
                            -1, 3 * chans
                        )
                        for tap in range(3)
                    ],
                    axis=1,
                )
                for window in (slice(0, 3 * chans), slice(chans, 4 * chans))
            ],
            axis=0,
        )
        return jnp.dot(lhs, weight_ref[...], preferred_element_type=F32)

    copies = []

    def finish(low, found):
        base = skipped_ref[low * cols : (low + 1) * cols, :]
        for side in range(2):
            row = 2 * low + side
            for phase in range(2):
                start = (2 * phase + side) * cols
                value = base + found[start : start + cols]
                for half in range(chans // LANES):
                    mixed_ref[row, half, pl.ds(phase, cols, stride=2), :] = value[
                        :, half * LANES : (half + 1) * LANES
                    ]
            for half in range(chans // LANES):
                done_ref[row, :, half * LANES : (half + 1) * LANES] = mixed_ref[row, half].astype(
                    BF16
                )
            copies.append(pltpu.make_async_copy(done_ref.at[row], out_ref.at[row], sems.at[row]))
            copies[-1].start()

    found = []
    filled = 0
    for low in range(rows // 2):
        for row in range(filled, 2 * low + 4):
            fill(row)
        filled = 2 * low + 4
        found.append(multiply(low))
    for low in range(rows // 2):
        finish(low, found[low])
    for copy in copies:
        copy.wait()


def exchange(values, axis):
    peers = lax.axis_size(axis)
    if peers & (peers - 1):
        return lax.psum(values, axis)
    step = 1
    while step < peers:
        radix = 2 if peers // step == 2 else 4
        parts = [
            lax.ppermute(values, axis, [(i, i ^ (step * k)) for i in range(peers)])
            for k in range(1, radix)
        ]
        values = sum(parts, values)
        step *= radix
    return values


def body(latent, gain_in, shift_in, conv_in, gain_mid, shift_mid, conv_mid, skip_weight):
    axis = "rows"
    peers = lax.axis_size(axis)
    rows, cols, chans = latent.shape
    outs = conv_in.shape[1]
    ends = peers - 1
    taken = vmem_spec()
    far = pl.BlockSpec(memory_space=pltpu.HBM)
    dma = pltpu.SemaphoreType.DMA
    whole = jax.ShapeDtypeStruct

    stats, near_row, far_row = pl.pallas_call(
        stats_kernel,
        out_shape=(
            whole((peers, 8, LANES), F32),
            whole((1, cols, chans), BF16),
            whole((1, cols, chans), BF16),
        ),
        in_specs=[far],
        out_specs=(taken,) * 3,
        scratch_shapes=[VMEM(latent.shape, BF16), dma((rows,))],
        compiler_params=params(16),
        name="stats",
    )(in_hbm(latent))
    inner = range(1, ends)
    far_row = lax.ppermute(far_row, axis, [(i, i + 1 if i % 2 else i - 1) for i in inner])
    stats = lax.all_to_all(stats, axis, 0, 0)
    near_row = lax.ppermute(near_row, axis, [(i, i ^ 1) for i in range(peers)])

    ready = [latent, gain_in.reshape(1, -1), shift_in.reshape(1, -1), conv_in]
    ready = pl.pallas_call(
        load_kernel,
        out_shape=[
            VMEM(latent.shape, BF16),
            VMEM((1, chans), F32),
            VMEM((1, chans), F32),
            VMEM(conv_in.shape, BF16),
        ],
        in_specs=[far] * 4,
        out_specs=[taken] * 4,
        scratch_shapes=[dma((4,))],
        compiler_params=params(4),
        cost_estimate=cost(4 << 20, 8 << 20),
        name="load",
    )(*map(in_hbm, ready))
    near_latent, near_gain, near_shift, near_conv = ready

    hidden, stats_mid, affine = pl.pallas_call(
        functools.partial(
            hidden_kernel, float(rows * cols * (chans // GROUPS) * peers), peers
        ),
        out_shape=(
            whole((2 * rows + 2, 2, cols, outs), BF16),
            whole((1, 8, LANES), F32),
            VMEM((2, 1, chans), F32),
        ),
        in_specs=[taken] * 7,
        out_specs=(taken,) * 3,
        scratch_shapes=[
            VMEM((rows + 2, cols, chans), BF16),
            VMEM((9, outs // LANES, (rows + 2) * (cols + GUARD) + GUARD, LANES), F32),
        ],
        compiler_params=params(24),
        name="hidden",
    )(
        stats,
        near_row,
        far_row,
        near_latent,
        near_gain,
        near_shift,
        near_conv,
    )
    stats_mid = exchange(stats_mid, axis)

    near_gain, near_shift, near_mid, skipped = pl.pallas_call(
        skip_kernel,
        out_shape=(
            VMEM((1, outs), F32),
            VMEM((1, outs), F32),
            VMEM(conv_mid.shape, BF16),
            whole((rows * cols, outs), F32),
        ),
        in_specs=[taken] + [far] * 5,
        out_specs=(taken,) * 4,
        scratch_shapes=[VMEM(latent.shape, BF16), VMEM((chans, outs), BF16), dma((5,))],
        compiler_params=params(16),
        cost_estimate=cost(200 << 20, 8 << 20),
        name="skip",
    )(
        affine,
        in_hbm(gain_mid.reshape(1, -1)),
        in_hbm(shift_mid.reshape(1, -1)),
        in_hbm(conv_mid),
        in_hbm(latent),
        in_hbm(skip_weight),
    )

    return pl.pallas_call(
        functools.partial(output_kernel, float(4 * rows * cols * (outs // GROUPS) * peers), peers),
        out_shape=whole((2 * rows, 2 * cols, outs), BF16),
        in_specs=[taken] * 6,
        out_specs=far,
        scratch_shapes=[
            VMEM((2 * rows + 2, cols, 4 * outs), BF16),
            VMEM((2 * rows, outs // LANES, 2 * cols, LANES), F32),
            VMEM((2 * rows, 2 * cols, outs), BF16),
            dma((2 * rows,)),
        ],
        compiler_params=params(24),
        name="output",
    )(stats_mid, hidden, near_gain, near_shift, near_mid, skipped)


def solution(mesh):
    placed = (P(("groups", "rows"), None, None), P(), P(), P(), P(), P(), P(), P())
    return jax.shard_map(
        body,
        mesh=mesh,
        in_specs=placed,
        out_specs=P(("groups", "rows"), None, None),
        check_vma=False,
    )
```
